128 devices in a mesh: row: 16 (over x, z), col: 8 (over y, core).
Axes of the slice: x: 4, y: 4, z: 4, core: 2. Of those that a mesh axis runs over, the one named last changes fastest.
Arguments:
- amplitudes: bfloat16 [1536, 64, 1024], P('row', 'col'), may hold values from -6 to 6
- integrals: bfloat16 [64, 1024, 16384], P('col', None, 'row'), may hold values from -0.03125 to 0.03125
- block_counts: int32 [8], replicated, may hold values from 1 to 8, 32 in all
Outputs:
- ladder: bfloat16 [1536, 16384], P('col', 'row')
The draws below stay inside these ranges and needn't reach their ends.
Inputs may be any that keep to these rules, and one draw needn't show every extreme that they name: Owner c holds its live blocks in its first block_counts[c] slots; the counts sum to 32 and the largest is exactly 8.
All inputs are finite; a program needn't handle non-finite values.
Results may differ from the reference program's by a relative error of at most 0.001.
Values may be sent and summed in bfloat16 or wider, within the bound.
No kernel may reach another device: no remote copies, remote signals or barrier semaphores. Data moves between devices by JAX's collectives and lax.ppermute only.
A program may use at most 128 MiB of HBM per device.

```python
import math
import jax
import jax.numpy as jnp
import numpy as np
from jax import lax

VIRTUAL_PAIRS = 16384
TILE_ENTRIES = 1024
SLOTS = 8
OCCUPIED_PAIRS = 1536
LIVE_BLOCKS = 32
BLOCK_SLOTS = 64
N_COL = 8


def shard_levels(rng, shape, cuts, low, largest):
    def one(dim, shards_of):
        draws = jax.random.uniform(jax.random.fold_in(jax.random.fold_in(rng, 6), dim), (shards_of,), jnp.float32, low / len(cuts), largest / len(cuts))
        return jnp.repeat(jnp.exp(draws), shape[dim] // shards_of).reshape((-1,) + (1,) * (len(shape) - dim - 1))

    gain = one(*cuts[0])
    for cut in cuts[1:]:
        gain = gain * one(*cut)
    return gain


def length_profile(count, total, limit, skew):
    portions = [(1 << 20) // math.isqrt(rank ** skew) + 1 for rank in range(2, count + 1)]
    spare, counts = total - limit - (count - 1), [1] * (count - 1)
    while spare > 0:
        candidates = [i for i in range(count - 1) if counts[i] < limit]
        mass, left = sum([portions[i] for i in candidates]), spare
        for i in candidates:
            addition = min(limit - counts[i], max(1, left * portions[i] // mass), spare)
            counts[i] = counts[i] + addition
            spare = spare - addition
    return np.array([limit] + counts)


def uneven(rng, count, total, most, skew):
    if count == 2:
        one = jax.random.randint(rng, (), max(1, total - most), min(most, total - 1) + 1)
        return jnp.stack([one, total - one])
    lengths = jnp.asarray(length_profile(count, total, most, skew), jnp.int32)
    twos = (count - 1) // 2
    donor, receiver = lengths[1:1 + 2 * twos:2], lengths[2:2 + 2 * twos:2]
    slack = jnp.minimum(donor - 1, most - receiver)
    shifted = jax.random.randint(jax.random.fold_in(rng, 1), (twos,), 0, 1 << 20) % (slack + 1)
    lengths = lengths.at[1:1 + 2 * twos:2].set(donor - shifted).at[2:2 + 2 * twos:2].set(receiver + shifted)
    return lengths[jax.random.permutation(jax.random.fold_in(rng, 2), count)]


def bell_draw(key, extent, deviation, most, shards=(), kind=jnp.bfloat16):
    loudness = shard_levels(key, extent, shards, -0.22, 0.18) if shards else 1.0
    values = jax.random.normal(key, extent, jnp.float32) * deviation * loudness
    return jnp.minimum(jnp.maximum(values, -most), most).astype(kind)


def setup_inputs(seed: int = 0) -> dict:
    seeds = jax.random.split(jax.random.key(seed), 4)
    amplitudes = bell_draw(seeds[0], (OCCUPIED_PAIRS, BLOCK_SLOTS, TILE_ENTRIES), 1.0, 6.0, ((0, 16), (1, 8)))
    integrals = bell_draw(seeds[1], (BLOCK_SLOTS, TILE_ENTRIES, VIRTUAL_PAIRS), (LIVE_BLOCKS * TILE_ENTRIES) ** -0.5, 0.03125, ((0, 8), (2, 16)))
    block_counts = uneven(seeds[2], N_COL, LIVE_BLOCKS, SLOTS, 2).astype(jnp.int32)
    return dict(amplitudes=amplitudes, integrals=integrals, block_counts=block_counts)


def reference(amplitudes, integrals, block_counts):
    block_ends = jnp.cumsum(block_counts).astype(jnp.int32)
    block_offsets = (block_ends - block_counts).astype(jnp.int32)
    live_order = jnp.arange(LIVE_BLOCKS, dtype=jnp.int32)
    owner_col = jnp.sum((live_order[:, None] >= block_ends[None, :]).astype(jnp.int32), axis=1).astype(jnp.int32)
    col_ids = jnp.arange(N_COL, dtype=jnp.int32)
    leading_live_block = jnp.sum(jnp.where(owner_col[:, None] == col_ids[None, :], block_offsets[None, :], 0), axis=1).astype(jnp.int32)
    slot_ids = (owner_col * SLOTS + live_order - leading_live_block).astype(jnp.int32)

    def add_block(running, slot_id):
        amp_slot = lax.dynamic_index_in_dim(amplitudes, slot_id, 1, keepdims=False)
        int_slot = lax.dynamic_index_in_dim(integrals, slot_id, 0, keepdims=False)
        return running + jnp.dot(amp_slot, int_slot, preferred_element_type=jnp.float32), None

    zero_sum = jnp.zeros((OCCUPIED_PAIRS, VIRTUAL_PAIRS), jnp.float32)
    running, unused = lax.scan(add_block, zero_sum, slot_ids)
    return running.astype(jnp.bfloat16)
```

```python
import functools
import jax
import jax.numpy as jnp
from jax import lax
from jax.experimental import pallas as pl
from jax.experimental.pallas import tpu as pltpu
from jax.sharding import PartitionSpec as P

SIZES = (10, 12, 14, 16)
CHUNKS = 3


def ring_x(d):
    return [(x * 4 + z, (x + d) % 4 * 4 + z) for x in range(4) for z in range(4)]


def ring_z(d):
    return [(x * 4 + z, x * 4 + (z + d) % 4) for x in range(4) for z in range(4)]


def ring_y(d):
    return [(y * 2 + c, (y + d) % 4 * 2 + c) for y in range(4) for c in range(2)]


SWAP = [(c, c ^ 1) for c in range(8)]


def scalars(block_counts):
    row, col = lax.axis_index("row"), lax.axis_index("col")
    x, z, y, k = row // 4, row % 4, col // 2, col % 2
    eight = lax.iota(jnp.int32, 8)
    own = jnp.sum(jnp.where(eight == col, block_counts, 0))
    other = jnp.sum(jnp.where(eight == (col ^ 1), block_counts, 0))
    i = lax.iota(jnp.int32, 16)

    def place(d):
        d = d % 4
        return jnp.where(d == 0, 0, jnp.where(d == 3, 1, jnp.where(d == 1, 2, 3)))

    v = jnp.where(i == 0, k, 0)
    v = jnp.where(i == 1, own, v)
    v = jnp.where(i == 2, other, v)
    v = jnp.where(i == 3, own + other, v)
    v = jnp.where((i >= 4) & (i < 8), place(y + i - 4 - x + 4), v)
    v = jnp.where((i >= 8) & (i < 12), place(i - 8 - z + 4), v)
    return v


def own_slot(j, s):
    return jnp.minimum(j, s[1] - 1)


def other_slot(j, s):
    return jnp.clip(j - s[1], 0, s[2] - 1)


def pack_kernel(m, s, own, other, *outs):
    j = pl.program_id(0)
    for h in range(2):
        for who, ref in ((0, own), (1, other)):

            @pl.when(((j < m // 2) if h == 0 else (j >= m // 2)) & ((j < s[1]) if who == 0 else (j >= s[1])))
            def _():
                for c in range(CHUNKS):
                    outs[h * CHUNKS + c][...] = ref[0, c * 16 : (c + 1) * 16, :]


def pack(m, s, own, other):
    half = m // 2
    return pl.pallas_call(
        functools.partial(pack_kernel, m),
        grid_spec=pltpu.PrefetchScalarGridSpec(
            num_scalar_prefetch=1,
            grid=(m,),
            in_specs=[
                pl.BlockSpec((1, 48, 1024), lambda j, s: (own_slot(j, s), 0, 0)),
                pl.BlockSpec((1, 48, 1024), lambda j, s: (other_slot(j, s), 0, 0)),
            ],
            out_specs=[pl.BlockSpec((16, 1024), lambda j, s: (0, jnp.minimum(j, half - 1)))] * CHUNKS
            + [pl.BlockSpec((16, 1024), lambda j, s: (0, jnp.maximum(j - half, 0)))] * CHUNKS,
        ),
        out_shape=[jax.ShapeDtypeStruct((16, half * 1024), jnp.bfloat16)] * (2 * CHUNKS),
        cost_estimate=pl.CostEstimate(flops=0, bytes_accessed=4 * 48 * 1024 * m, transcendentals=0),
        name="pack",
    )(s, own, other)


def multiply_kernel(m, s, *refs):
    lhs, (own, other), outs, (stage, held, total, sems) = refs[:16], refs[16:18], refs[18:22], refs[22:]
    half = m // 2
    mine, live = s[1], s[3]

    def copy(j, slot, start):
        for which, ref in ((0, own), (1, other)):

            @pl.when((j < mine) if which == 0 else (j >= mine))
            def _():
                index = j if which == 0 else j - mine
                block = pltpu.make_async_copy(ref.at[index], held.at[slot], sems.at[slot])
                block.start() if start else block.wait()

    total[...] = jnp.zeros_like(total)
    copy(0, 0, True)

    def step(j, carry):
        slot = j % 2

        @pl.when(j + 1 < live)
        def _():
            copy(j + 1, 1 - slot, True)

        for h in range(2):

            @pl.when((j < half) if h == 0 else (j >= half))
            def _():
                columns = pl.ds(pl.multiple_of((j - h * half) * 1024, 1024), 1024)
                for far in range(4):
                    for near in range(4):
                        ref = lhs[h * 8 + far * 2 + near // 2]
                        dx, dz = (near, far) if h == 0 else (far, near)
                        at = dx * 64 + dz * 16
                        stage[at : at + 16, :] = ref[near % 2 * 16 : near % 2 * 16 + 16, columns]

        copy(j, slot, False)

        @pl.loop(0, 4)
        def _(n):
            columns = pl.ds(pl.multiple_of(n * 256, 256), 256)
            total[:, columns] += jnp.dot(stage[...], held[slot, :, columns], preferred_element_type=jnp.float32)

        return carry

    lax.fori_loop(0, live, step, 0)
    for dy in range(4):
        at = pl.multiple_of(s[4 + dy] * 64, 64)
        outs[dy][...] = total[pl.ds(at, 64), :]


def multiply(m, s, lhs, own, other):
    vmem, hbm = pl.BlockSpec(memory_space=pltpu.VMEM), pl.BlockSpec(memory_space=pl.ANY)
    return pl.pallas_call(
        functools.partial(multiply_kernel, m),
        in_specs=[pl.BlockSpec(memory_space=pltpu.SMEM)] + [vmem] * 16 + [hbm] * 2,
        out_specs=[vmem] * 4,
        scratch_shapes=[
            pltpu.VMEM((256, 1024), jnp.bfloat16),
            pltpu.VMEM((2, 1024, 1024), jnp.bfloat16),
            pltpu.VMEM((256, 1024), jnp.float32),
            pltpu.SemaphoreType.DMA((2,)),
        ],
        out_shape=[jax.ShapeDtypeStruct((64, 1024), jnp.float32)] * 4,
        compiler_params=pltpu.CompilerParams(vmem_limit_bytes=32 << 20),
        cost_estimate=pl.CostEstimate(
            flops=2 * 256 * 1024 * 1024 * m, bytes_accessed=m * (2 << 20) + 512 * 1024 * m, transcendentals=0
        ),
        name="multiply",
    )(s, *lhs, own, other)


def finish_kernel(s, a, b, c, d, keep, give):
    k = s[0]
    for i in range(2):
        for ref, core in ((keep, k), (give, 1 - k)):
            at = pl.ds(pl.multiple_of(s[8 + 2 * core + i] * 16, 16), 16)
            ref[i] = (a[at, :] + b[at, :] + c[at, :] + d[at, :]).astype(jnp.bfloat16)


def finish(s, parts):
    return pl.pallas_call(
        finish_kernel,
        in_specs=[pl.BlockSpec(memory_space=pltpu.SMEM)] + [pl.BlockSpec(memory_space=pltpu.VMEM)] * 4,
        out_specs=[pl.BlockSpec(memory_space=pltpu.VMEM)] * 2,
        out_shape=[jax.ShapeDtypeStruct((2, 16, 1024), jnp.bfloat16)] * 2,
        name="finish",
    )(s, *parts)


def gather(shard, near, far):
    left = lax.ppermute(shard, "row", near(1))
    right = lax.ppermute(shard, "row", near(3))
    across = lax.ppermute(shard, "row", near(2))
    one = jnp.concatenate([shard, left])
    two = jnp.concatenate([right, across])
    one_l, one_r = lax.ppermute(one, "row", far(1)), lax.ppermute(one, "row", far(3))
    two_r, two_l = lax.ppermute(two, "row", far(3)), lax.ppermute(two, "row", far(1))
    one_a = lax.ppermute(one_l, "row", far(1))
    two_a = lax.ppermute(two_r, "row", far(3))
    return [one, two, one_l, two_l, one_r, two_r, one_a, two_a]


def body(m, s, own, other, integrals):
    other_integrals = lax.ppermute(integrals, "col", SWAP)
    shards = pack(m, s, own, other)
    kept, given = [], []
    for c in range(CHUNKS):
        lhs = gather(shards[c], ring_x, ring_z) + gather(shards[CHUNKS + c], ring_z, ring_x)
        parts = multiply(m, s, lhs, integrals, other_integrals)
        parts = [parts[0]] + [lax.ppermute(parts[d], "col", ring_y(d)) for d in (1, 2, 3)]
        keep, give = finish(s, parts)
        kept.append(keep)
        given.append(lax.ppermute(give, "col", SWAP))
    mine, theirs = jnp.stack(kept, 1), jnp.stack(given, 1)
    mine, theirs = mine.reshape(2, 48, 1024), theirs.reshape(2, 48, 1024)
    low = s[0] == 0
    return jnp.stack([jnp.where(low, mine, theirs), jnp.where(low, theirs, mine)], 1).reshape(192, 1024)


def local(amplitudes, integrals, block_counts):
    k = lax.axis_index("col") % 2
    s = scalars(block_counts)
    give = lax.dynamic_slice_in_dim(amplitudes, 48 * (1 - k), 48, 0)
    other = lax.ppermute(give, "col", SWAP).transpose(1, 0, 2)
    own = lax.dynamic_slice_in_dim(amplitudes, 48 * k, 48, 0).transpose(1, 0, 2)
    largest = jnp.max(jnp.sum(block_counts.reshape(4, 2), axis=1))
    which = sum((largest > size).astype(jnp.int32) for size in SIZES[:-1])
    return lax.switch(which, [functools.partial(body, m) for m in SIZES], s, own, other, integrals)


def solution(mesh):
    return jax.shard_map(
        local,
        mesh=mesh,
        in_specs=(P("row", "col", None), P("col", None, "row"), P()),
        out_specs=P("col", "row"),
        check_vma=False,
    )
```

```python
import functools
import jax
import jax.numpy as jnp
from jax import lax
from jax.experimental import pallas as pl
from jax.experimental.pallas import tpu as pltpu
from jax.sharding import PartitionSpec as P

SIZES = (10, 12, 14, 16)
ROWS = (32, 16)
STARTS = (0, 32)
tie = lax.optimization_barrier


def ring_x(d):
    return [(x * 4 + z, (x + d) % 4 * 4 + z) for x in range(4) for z in range(4)]


def ring_z(d):
    return [(x * 4 + z, x * 4 + (z + d) % 4) for x in range(4) for z in range(4)]


def ring_y(d):
    return [(y * 2 + c, (y + d) % 4 * 2 + c) for y in range(4) for c in range(2)]


SWAP = [(c, c ^ 1) for c in range(8)]


def scalars(block_counts):
    row, col = lax.axis_index("row"), lax.axis_index("col")
    x, z, y, k = row >> 2, row & 3, col >> 1, col & 1
    eight = lax.iota(jnp.int32, 8)
    own = jnp.sum(jnp.where(eight == col, block_counts, 0))
    other = jnp.sum(jnp.where(eight == (col ^ 1), block_counts, 0))
    i = lax.iota(jnp.int32, 16)

    def place(d):
        d = d & 3
        return jnp.where(d == 0, 0, jnp.where(d == 3, 1, jnp.where(d == 1, 2, 3)))

    v = jnp.where(i == 0, k, 0)
    v = jnp.where(i == 1, own, v)
    v = jnp.where(i == 2, other, v)
    v = jnp.where(i == 3, own + other, v)
    v = jnp.where((i >= 4) & (i < 8), place(y + i - 4 - x + 4), v)
    v = jnp.where((i >= 8) & (i < 12), place(i - 8 - z + 4), v)
    return v


def pack_kernel(m, s, own, other, *outs):
    half = m // 2
    mine, live = s[1], s[3]
    for which, ref in ((0, own), (1, other)):
        for h in range(2):
            low = h * half if which == 0 else jnp.maximum(mine, h * half)
            high = jnp.minimum(mine if which == 0 else live, (h + 1) * half)

            @pl.loop(low, high)
            def _(j):
                columns = pl.ds(pl.multiple_of((j - h * half) * 1024, 1024), 1024)
                block = ref[j if which == 0 else j - mine]
                for c in range(len(ROWS)):
                    outs[h * len(ROWS) + c][:, columns] = block[STARTS[c] : STARTS[c] + ROWS[c]]


def pack(m, s, own, other):
    vmem = pl.BlockSpec(memory_space=pltpu.VMEM)
    return pl.pallas_call(
        functools.partial(pack_kernel, m),
        in_specs=[pl.BlockSpec(memory_space=pltpu.SMEM), vmem, vmem],
        out_specs=[vmem] * (2 * len(ROWS)),
        out_shape=[jax.ShapeDtypeStruct((rows, m * 512), jnp.bfloat16) for rows in ROWS * 2],
        compiler_params=pltpu.CompilerParams(vmem_limit_bytes=16 << 20),
        cost_estimate=pl.CostEstimate(flops=0, bytes_accessed=4 * 48 * 1024 * m, transcendentals=0),
        name="pack",
    )(s, own, other)


def multiply_kernel(m, rows, s, *refs):
    lhs, (own, other), outs, (stage, held, total, sems) = refs[:10], refs[10:12], refs[12:16], refs[16:]
    half = m // 2
    mine, live = s[1], s[3]

    def copy(j, slot, start):
        for which, ref in ((0, own), (1, other)):

            @pl.when((j < mine) if which == 0 else (j >= mine))
            def _():
                index = j if which == 0 else j - mine
                block = pltpu.make_async_copy(ref.at[index], held.at[slot], sems.at[slot])
                block.start() if start else block.wait()

    copy(0, 0, True)
    total[...] = jnp.zeros_like(total)

    def step(j, carry):
        slot = j % 2

        @pl.when(j + 1 < live)
        def _():
            copy(j + 1, 1 - slot, True)

        for h in range(2):

            @pl.when((j < half) if h == 0 else (j >= half))
            def _():
                columns = pl.ds(pl.multiple_of((j - h * half) * 1024, 1024), 1024)
                for far in range(4):
                    for near in range(4):
                        if far < 3:
                            ref, at = lhs[h * 5 + far], near * rows
                        else:
                            ref, at = lhs[h * 5 + 3 + near // 2], near % 2 * rows
                        dx, dz = (near, far) if h == 0 else (far, near)
                        to = (dx * 4 + dz) * rows
                        stage[to : to + rows, :] = ref[at : at + rows, columns]

        copy(j, slot, False)
        total[...] += jnp.dot(stage[...], held[slot], preferred_element_type=jnp.float32)
        return carry

    lax.fori_loop(0, live, step, 0)
    for dy in range(4):
        at = pl.multiple_of(s[4 + dy] * 4 * rows, 4 * rows)
        outs[dy][...] = total[pl.ds(at, 4 * rows), :]


def multiply(m, rows, s, lhs, own, other):
    vmem, hbm = pl.BlockSpec(memory_space=pltpu.VMEM), pl.BlockSpec(memory_space=pl.ANY)
    return pl.pallas_call(
        functools.partial(multiply_kernel, m, rows),
        in_specs=[pl.BlockSpec(memory_space=pltpu.SMEM)] + [vmem] * 10 + [hbm] * 2,
        out_specs=[vmem] * 4,
        scratch_shapes=[
            pltpu.VMEM((16 * rows, 1024), jnp.bfloat16),
            pltpu.VMEM((2, 1024, 1024), jnp.bfloat16),
            pltpu.VMEM((16 * rows, 1024), jnp.float32),
            pltpu.SemaphoreType.DMA((2,)),
        ],
        out_shape=[jax.ShapeDtypeStruct((4 * rows, 1024), jnp.float32)] * 4,
        compiler_params=pltpu.CompilerParams(vmem_limit_bytes=40 << 20),
        cost_estimate=pl.CostEstimate(
            flops=32 * rows * 1024 * 1024 * m, bytes_accessed=m * (2 << 20) + 32 * rows * 1024 * m, transcendentals=0
        ),
        name="multiply",
    )(s, *lhs, own, other)


def finish_kernel(rows, s, a, b, c, d, keep, give):
    k = s[0]
    for i in range(2):
        for ref, core in ((keep, k), (give, 1 - k)):
            at = pl.ds(pl.multiple_of(s[8 + 2 * core + i] * rows, rows), rows)
            ref[i] = (a[at, :] + b[at, :] + c[at, :] + d[at, :]).astype(jnp.bfloat16)


def finish(rows, s, parts):
    return pl.pallas_call(
        functools.partial(finish_kernel, rows),
        in_specs=[pl.BlockSpec(memory_space=pltpu.SMEM)] + [pl.BlockSpec(memory_space=pltpu.VMEM)] * 4,
        out_specs=[pl.BlockSpec(memory_space=pltpu.VMEM)] * 2,
        out_shape=[jax.ShapeDtypeStruct((2, rows, 1024), jnp.bfloat16)] * 2,
        compiler_params=pltpu.CompilerParams(vmem_limit_bytes=16 << 20),
        name="finish",
    )(s, *parts)


def first(shard, ring):
    return [shard] + [lax.ppermute(shard, "row", ring(d)) for d in (1, 3, 2)]


def second(line, ring):
    return lax.ppermute(line, "row", ring(1)), lax.ppermute(line, "row", ring(3))


def third(left, right, ring):
    half = left.shape[0] // 2
    return lax.ppermute(left[:half], "row", ring(1)), lax.ppermute(right[half:], "row", ring(3))


def spread(parts, s):
    return [parts[0]] + [lax.ppermute(parts[d], "col", ring_y(d)) for d in (1, 2, 3)]


def body(m, s, own, other, integrals):
    other_integrals = lax.ppermute(integrals, "col", SWAP)
    shards = pack(m, s, own, other)
    rings = ((ring_x, ring_z), (ring_z, ring_x))
    near = [first(shards[h * 2], rings[h][0]) for h in range(2)]
    lines = [jnp.concatenate(n) for n in near]
    lines, late = tie((lines, [shards[1], shards[3]]))
    wide = [second(lines[h], rings[h][1]) for h in range(2)]
    near_late = [first(late[h], rings[h][0]) for h in range(2)]
    lines_late = [jnp.concatenate(n) for n in near_late]
    wide, lines_late = tie((wide, lines_late))
    across = [third(*wide[h], rings[h][1]) for h in range(2)]
    wide_late = [second(lines_late[h], rings[h][1]) for h in range(2)]
    lhs = [v for h in range(2) for v in (lines[h], *wide[h], *across[h])]
    parts = multiply(m, ROWS[0], s, lhs, integrals, other_integrals)
    parts, wide_late = tie((parts, wide_late))
    across_late = [third(*wide_late[h], rings[h][1]) for h in range(2)]
    parts = spread(parts, s)
    keep0, give0 = finish(ROWS[0], s, parts)
    got0 = lax.ppermute(give0, "col", SWAP)
    lhs = [v for h in range(2) for v in (lines_late[h], *wide_late[h], *across_late[h])]
    parts = spread(multiply(m, ROWS[1], s, lhs, integrals, other_integrals), s)
    keep1, give1 = finish(ROWS[1], s, parts)
    got1 = lax.ppermute(give1, "col", SWAP)
    mine, theirs = jnp.concatenate([keep0, keep1], 1), jnp.concatenate([got0, got1], 1)
    low = s[0] == 0
    return jnp.stack([jnp.where(low, mine, theirs), jnp.where(low, theirs, mine)], 1).reshape(192, 1024)


def local(amplitudes, integrals, block_counts):
    k = lax.axis_index("col") & 1
    give = lax.dynamic_slice_in_dim(amplitudes, 48 * (1 - k), 48, 0)
    other = lax.ppermute(give, "col", SWAP).transpose(1, 0, 2)
    own = lax.dynamic_slice_in_dim(amplitudes, 48 * k, 48, 0).transpose(1, 0, 2)
    largest = jnp.max(jnp.sum(block_counts.reshape(4, 2), axis=1))
    which = sum((largest > size).astype(jnp.int32) for size in SIZES[:-1])
    s, own, other, which = tie((scalars(block_counts), own, other, which))
    return lax.switch(which, [functools.partial(body, m) for m in SIZES], s, own, other, integrals)


def solution(mesh):
    return jax.shard_map(
        local,
        mesh=mesh,
        in_specs=(P("row", "col", None), P("col", None, "row"), P()),
        out_specs=P("col", "row"),
        check_vma=False,
    )
```

```python
import functools
import jax
import jax.numpy as jnp
from jax import lax
from jax.experimental import pallas as pl
from jax.experimental.pallas import tpu as pltpu
from jax.sharding import PartitionSpec as P

SIZES = (10, 12)
ROWS = (32, 16)
STARTS = (0, 32)
tie = lax.optimization_barrier


def ring_x(d):
    return [(x * 4 + z, (x + d) % 4 * 4 + z) for x in range(4) for z in range(4)]


def ring_z(d):
    return [(x * 4 + z, x * 4 + (z + d) % 4) for x in range(4) for z in range(4)]


def ring_y(d):
    return [(y * 2 + c, (y + d) % 4 * 2 + c) for y in range(4) for c in range(2)]


SWAP = [(c, c ^ 1) for c in range(8)]


def plan_kernel(row, col, counts, s):
    row, col = row[0], col[0]
    x, z, y, k = row >> 2, row & 3, col >> 1, col & 1
    index = lax.broadcasted_iota(jnp.int32, (32, 128), 0) * 128 + lax.broadcasted_iota(jnp.int32, (32, 128), 1)
    flow = [((index >> (3 * e)) & 7) - 2 for e in range(4)]
    most, moved = jnp.zeros((32, 128), jnp.int32), jnp.zeros((32, 128), jnp.int32)
    for e in range(4):
        a, b = counts[2 * e], counts[2 * e + 1]
        most = jnp.maximum(most, a + b - flow[e] + flow[(e + 3) % 4])
        moved += jnp.abs(flow[e])
        down = -flow[(e + 3) % 4]
        allowed = jnp.where(jnp.minimum(a, b) >= 2, 2, jnp.where(jnp.maximum(a, b) >= 2, 1, 0))
        most = jnp.where((flow[e] > 2) | (down > allowed), 31, most)
    best = jnp.min((most * 131072 + moved * 4096 + index).astype(jnp.float32)).astype(jnp.int32)
    largest = best >> 17

    def sends(y, k):
        y = y & 3
        n, other = counts[2 * y + k], counts[2 * y + 1 - k]
        chosen = (n > other) | ((n == other) & (k == 0))
        up = ((best >> (3 * y)) & 7) - 2
        down = 2 - ((best >> (3 * ((y + 3) & 3))) & 7)
        return [jnp.where((v == 2) | ((v == 1) & chosen), 1, 0) for v in (up, down)]

    def place(d):
        d = d & 3
        return jnp.where(d == 0, 0, jnp.where(d == 3, 1, jnp.where(d == 1, 2, 3)))

    mine, others = sends(y, k), sends(y, 1 - k)
    s[0] = k
    s[1] = counts[col] - mine[0] - mine[1]
    s[2] = s[1] + counts[col ^ 1] - others[0] - others[1]
    s[3] = s[2] + sends(y + 3, k)[0]
    s[4] = s[3] + sends(y + 3, 1 - k)[0]
    s[5] = s[4] + sends(y + 1, k)[1]
    s[6] = s[5] + sends(y + 1, 1 - k)[1]
    s[7] = sum(jnp.where(largest > size, 1, 0) for size in SIZES[:-1])
    for d in range(4):
        s[8 + d] = place(y + d - x + 4)
        s[12 + d] = place(d - z + 4)
    s[16], s[17], s[18], s[19] = *mine, *others


def plan(block_counts):
    smem = pl.BlockSpec(memory_space=pltpu.SMEM)
    return pl.pallas_call(
        plan_kernel,
        in_specs=[smem] * 3,
        out_specs=smem,
        out_shape=jax.ShapeDtypeStruct((20,), jnp.int32),
        name="plan",
    )(lax.axis_index("row")[None], lax.axis_index("col")[None], block_counts)


def sources(s, j):
    def kept(j, up, down):
        return j + jnp.where(up == 1, 1 + down, jnp.where(j >= 1, down, 0))

    yield 0, j < s[1], kept(j, s[16], s[17])
    yield 1, (j >= s[1]) & (j < s[2]), kept(j - s[1], s[18], s[19])
    for i in range(2, 6):
        yield i, (j >= s[i]) & (j < s[i + 1]), 0


def pack_kernel(m, s, *refs):
    blocks, outs = refs[:6], refs[6:]
    half = m // 2

    @pl.loop(0, s[6])
    def _(j):
        for i, here, slot in sources(s, j):
            for h in range(2):

                @pl.when(here & ((j < half) if h == 0 else (j >= half)))
                def _():
                    columns = pl.ds(pl.multiple_of((j - h * half) * 1024, 1024), 1024)
                    outs[h][:, columns] = blocks[i][slot]


def pack(m, s, blocks):
    vmem = pl.BlockSpec(memory_space=pltpu.VMEM)
    return pl.pallas_call(
        functools.partial(pack_kernel, m),
        in_specs=[pl.BlockSpec(memory_space=pltpu.SMEM)] + [vmem] * 6,
        out_specs=[vmem] * 2,
        out_shape=[jax.ShapeDtypeStruct((48, m * 512), jnp.bfloat16)] * 2,
        compiler_params=pltpu.CompilerParams(vmem_limit_bytes=16 << 20),
        cost_estimate=pl.CostEstimate(flops=0, bytes_accessed=4 * 48 * 1024 * m, transcendentals=0),
        name="pack",
    )(s, *blocks)


def multiply_kernel(m, rows, s, *refs):
    lhs, blocks, outs, (stage, held, total, sems) = refs[:10], refs[10:16], refs[16:20], refs[20:]
    half = m // 2
    live = s[6]

    def start(j, slot):
        for i, here, index in sources(s, j):

            @pl.when(here)
            def _():
                pltpu.make_async_copy(blocks[i].at[index], held.at[slot], sems.at[slot]).start()

    start(0, 0)
    total[...] = jnp.zeros_like(total)

    def step(j, carry):
        slot = j % 2

        @pl.when(j + 1 < live)
        def _():
            start(j + 1, 1 - slot)

        for h in range(2):

            @pl.when((j < half) if h == 0 else (j >= half))
            def _():
                columns = pl.ds(pl.multiple_of((j - h * half) * 1024, 1024), 1024)
                for far in range(4):
                    for near in range(4):
                        if far < 3:
                            ref, at = lhs[h * 5 + far], near * rows
                        else:
                            ref, at = lhs[h * 5 + 3 + near // 2], near % 2 * rows
                        dx, dz = (near, far) if h == 0 else (far, near)
                        to = (dx * 4 + dz) * rows
                        stage[to : to + rows, :] = ref[at : at + rows, columns]

        pltpu.make_async_copy(blocks[0].at[0], held.at[slot], sems.at[slot]).wait()
        total[...] += jnp.dot(stage[...], held[slot], preferred_element_type=jnp.float32)
        return carry

    lax.fori_loop(0, live, step, 0)
    for dy in range(4):
        at = pl.multiple_of(s[8 + dy] * 4 * rows, 4 * rows)
        outs[dy][...] = total[pl.ds(at, 4 * rows), :]


def multiply(m, rows, s, lhs, blocks):
    vmem, hbm = pl.BlockSpec(memory_space=pltpu.VMEM), pl.BlockSpec(memory_space=pl.ANY)
    return pl.pallas_call(
        functools.partial(multiply_kernel, m, rows),
        in_specs=[pl.BlockSpec(memory_space=pltpu.SMEM)] + [vmem] * 10 + [hbm] * 6,
        out_specs=[vmem] * 4,
        scratch_shapes=[
            pltpu.VMEM((16 * rows, 1024), jnp.bfloat16),
            pltpu.VMEM((2, 1024, 1024), jnp.bfloat16),
            pltpu.VMEM((16 * rows, 1024), jnp.float32),
            pltpu.SemaphoreType.DMA((2,)),
        ],
        out_shape=[jax.ShapeDtypeStruct((4 * rows, 1024), jnp.float32)] * 4,
        compiler_params=pltpu.CompilerParams(vmem_limit_bytes=40 << 20),
        cost_estimate=pl.CostEstimate(
            flops=32 * rows * 1024 * 1024 * m, bytes_accessed=m * (2 << 20) + 32 * rows * 1024 * m, transcendentals=0
        ),
        name="multiply",
    )(s, *lhs, *blocks)


def finish_kernel(rows, s, a, b, c, d, keep, give):
    k = s[0]
    for i in range(2):
        for ref, core in ((keep, k), (give, 1 - k)):
            at = pl.ds(pl.multiple_of(s[12 + 2 * core + i] * rows, rows), rows)
            ref[i] = (a[at, :] + b[at, :] + c[at, :] + d[at, :]).astype(jnp.bfloat16)


def finish(rows, s, parts):
    return pl.pallas_call(
        functools.partial(finish_kernel, rows),
        in_specs=[pl.BlockSpec(memory_space=pltpu.SMEM)] + [pl.BlockSpec(memory_space=pltpu.VMEM)] * 4,
        out_specs=[pl.BlockSpec(memory_space=pltpu.VMEM)] * 2,
        out_shape=[jax.ShapeDtypeStruct((2, rows, 1024), jnp.bfloat16)] * 2,
        compiler_params=pltpu.CompilerParams(vmem_limit_bytes=16 << 20),
        name="finish",
    )(s, *parts)


def first(shard, ring):
    return [shard] + [lax.ppermute(shard, "row", ring(d)) for d in (1, 3, 2)]


def second(line, ring):
    return lax.ppermute(line, "row", ring(1)), lax.ppermute(line, "row", ring(3))


def third(left, right, ring):
    half = left.shape[0] // 2
    return lax.ppermute(left[:half], "row", ring(1)), lax.ppermute(right[half:], "row", ring(3))


def spread(parts, s):
    return [parts[0]] + [lax.ppermute(parts[d], "col", ring_y(d)) for d in (1, 2, 3)]


def body(m, s, integrals, *blocks):
    other_integrals = lax.ppermute(integrals, "col", SWAP)
    shards, give = tie((pack(m, s, blocks), [integrals[:1], integrals[1:2]]))
    moved = [lax.ppermute(v, "col", ring_y(d)) for v, d in zip(give, (1, 3))]
    rings = ((ring_x, ring_z), (ring_z, ring_x))
    near = [first(shards[h], rings[h][0]) for h in range(2)]
    lines = [[jnp.concatenate([v[a : a + n] for v in near[h]]) for h in range(2)] for a, n in zip(STARTS, ROWS)]
    wide = [second(lines[0][h], rings[h][1]) for h in range(2)]
    wide, late, moved = tie((wide, lines[1], moved))
    across = [third(*wide[h], rings[h][1]) for h in range(2)]
    wide_late = [second(late[h], rings[h][1]) for h in range(2)]
    swapped = [lax.ppermute(v, "col", SWAP) for v in moved]
    blocks = [integrals, other_integrals, moved[0], swapped[0], moved[1], swapped[1]]
    lhs = [v for h in range(2) for v in (lines[0][h], *wide[h], *across[h])]
    parts = multiply(m, ROWS[0], s, lhs, blocks)
    parts, wide_late = tie((parts, wide_late))
    across_late = [third(*wide_late[h], rings[h][1]) for h in range(2)]
    keep0, give0 = finish(ROWS[0], s, spread(parts, s))
    lhs = [v for h in range(2) for v in (late[h], *wide_late[h], *across_late[h])]
    keep1, give1 = finish(ROWS[1], s, spread(multiply(m, ROWS[1], s, lhs, blocks), s))
    mine = jnp.concatenate([keep0, keep1], 1)
    theirs = lax.ppermute(jnp.concatenate([give0, give1], 1), "col", SWAP)
    low = s[0] == 0
    return jnp.stack([jnp.where(low, mine, theirs), jnp.where(low, theirs, mine)], 1).reshape(192, 1024)


def local(amplitudes, integrals, block_counts):
    k = lax.axis_index("col") & 1
    give = lax.dynamic_slice_in_dim(amplitudes, 48 * (1 - k), 48, 0).transpose(1, 0, 2)
    other = lax.ppermute(give, "col", SWAP)
    own = lax.dynamic_slice_in_dim(amplitudes, 48 * k, 48, 0).transpose(1, 0, 2)
    blocks = [own, other]
    for i, d in ((0, 1), (1, 3)):
        blocks.append(lax.ppermute(own[i : i + 1], "col", ring_y(d)))
        blocks.append(lax.ppermute(give[i : i + 1], "col", [(a, b ^ 1) for a, b in ring_y(d)]))
    s = plan(block_counts)
    return lax.switch(s[7], [functools.partial(body, m) for m in SIZES], s, integrals, *blocks)


def solution(mesh):
    return jax.shard_map(
        local,
        mesh=mesh,
        in_specs=(P("row", "col", None), P("col", None, "row"), P()),
        out_specs=P("col", "row"),
        check_vma=False,
    )
```

```python
import functools
import jax
import jax.numpy as jnp
from jax import lax
from jax.experimental import pallas as pl
from jax.experimental.pallas import tpu as pltpu
from jax.sharding import PartitionSpec as P

SIZES = (10, 12)
ROWS = (32, 16)
STARTS = (0, 32)
tie = lax.optimization_barrier


def ring_x(d):
    return [(x * 4 + z, (x + d) % 4 * 4 + z) for x in range(4) for z in range(4)]


def ring_z(d):
    return [(x * 4 + z, x * 4 + (z + d) % 4) for x in range(4) for z in range(4)]


def ring_y(d):
    return [(y * 2 + c, (y + d) % 4 * 2 + c) for y in range(4) for c in range(2)]


SWAP = [(c, c ^ 1) for c in range(8)]


def plan_kernel(row, col, counts, s):
    row, col = row[0], col[0]
    x, z, y, k = row >> 2, row & 3, col >> 1, col & 1
    index = lax.broadcasted_iota(jnp.int32, (32, 128), 0) * 128 + lax.broadcasted_iota(jnp.int32, (32, 128), 1)
    flow = [((index >> (3 * e)) & 7) - 2 for e in range(4)]
    most, moved = jnp.zeros((32, 128), jnp.int32), jnp.zeros((32, 128), jnp.int32)
    for e in range(4):
        a, b = counts[2 * e], counts[2 * e + 1]
        most = jnp.maximum(most, a + b - flow[e] + flow[(e + 3) % 4])
        moved += jnp.abs(flow[e])
        down = -flow[(e + 3) % 4]
        allowed = jnp.where(jnp.minimum(a, b) >= 2, 2, jnp.where(jnp.maximum(a, b) >= 2, 1, 0))
        most = jnp.where((flow[e] > 2) | (down > allowed), 31, most)
    best = jnp.min((most * 131072 + moved * 4096 + index).astype(jnp.float32)).astype(jnp.int32)
    largest = best >> 17

    def sends(y, k):
        y = y & 3
        n, other = counts[2 * y + k], counts[2 * y + 1 - k]
        chosen = (n > other) | ((n == other) & (k == 0))
        up = ((best >> (3 * y)) & 7) - 2
        down = 2 - ((best >> (3 * ((y + 3) & 3))) & 7)
        return [jnp.where((v == 2) | ((v == 1) & chosen), 1, 0) for v in (up, down)]

    def place(d):
        d = d & 3
        return jnp.where(d == 0, 0, jnp.where(d == 3, 1, jnp.where(d == 1, 2, 3)))

    mine, others = sends(y, k), sends(y, 1 - k)
    s[0] = k
    s[1] = counts[col] - mine[0] - mine[1]
    s[2] = s[1] + counts[col ^ 1] - others[0] - others[1]
    s[3] = s[2] + sends(y + 3, k)[0]
    s[4] = s[3] + sends(y + 3, 1 - k)[0]
    s[5] = s[4] + sends(y + 1, k)[1]
    s[6] = s[5] + sends(y + 1, 1 - k)[1]
    s[7] = sum(jnp.where(largest > size, 1, 0) for size in SIZES[:-1])
    for d in range(4):
        s[8 + d] = place(y + d - x + 4)
        s[12 + d] = place(d - z + 4)
    s[16], s[17], s[18], s[19] = *mine, *others


def plan(block_counts):
    smem = pl.BlockSpec(memory_space=pltpu.SMEM)
    return pl.pallas_call(
        plan_kernel,
        in_specs=[smem] * 3,
        out_specs=smem,
        out_shape=jax.ShapeDtypeStruct((20,), jnp.int32),
        name="plan",
    )(lax.axis_index("row")[None], lax.axis_index("col")[None], block_counts)


def sources(s, j):
    def kept(j, up, down):
        return j + jnp.where(up == 1, 1 + down, jnp.where(j >= 1, down, 0))

    yield 0, j < s[1], kept(j, s[16], s[17])
    yield 1, (j >= s[1]) & (j < s[2]), kept(j - s[1], s[18], s[19])
    for i in range(2, 6):
        yield i, (j >= s[i]) & (j < s[i + 1]), 0


def pack_kernel(m, s, *refs):
    blocks, outs = refs[:6], refs[6:]
    half = m // 2

    @pl.loop(0, s[6])
    def _(j):
        for i, here, slot in sources(s, j):
            for h in range(2):

                @pl.when(here & ((j < half) if h == 0 else (j >= half)))
                def _():
                    columns = pl.ds(pl.multiple_of((j - h * half) * 1024, 1024), 1024)
                    outs[h][:, columns] = blocks[i][slot]


def pack(m, s, blocks):
    vmem = pl.BlockSpec(memory_space=pltpu.VMEM)
    return pl.pallas_call(
        functools.partial(pack_kernel, m),
        in_specs=[pl.BlockSpec(memory_space=pltpu.SMEM)] + [vmem] * 6,
        out_specs=[vmem] * 2,
        out_shape=[jax.ShapeDtypeStruct((48, m * 512), jnp.bfloat16)] * 2,
        compiler_params=pltpu.CompilerParams(vmem_limit_bytes=16 << 20),
        cost_estimate=pl.CostEstimate(flops=0, bytes_accessed=4 * 48 * 1024 * m, transcendentals=0),
        name="pack",
    )(s, *blocks)


def multiply_kernel(m, rows, s, *refs):
    lhs, blocks, outs, (stage, held, total, sems) = refs[:10], refs[10:16], refs[16:20], refs[20:]
    half = m // 2
    live = s[6]

    def start(j, slot):
        for i, here, index in sources(s, j):

            @pl.when(here)
            def _():
                pltpu.make_async_copy(blocks[i].at[index], held.at[slot], sems.at[slot]).start()

    for j in range(3):

        @pl.when(j < live)
        def _():
            start(j, j)

    total[...] = jnp.zeros_like(total)

    def step(j, carry):
        slot = j & 3

        @pl.when(j + 3 < live)
        def _():
            start(j + 3, (j + 3) & 3)

        for h in range(2):

            @pl.when((j < half) if h == 0 else (j >= half))
            def _():
                columns = pl.ds(pl.multiple_of((j - h * half) * 1024, 1024), 1024)
                for far in range(4):
                    for near in range(4):
                        if far < 3:
                            ref, at = lhs[h * 5 + far], near * rows
                        else:
                            ref, at = lhs[h * 5 + 3 + near // 2], near % 2 * rows
                        dx, dz = (near, far) if h == 0 else (far, near)
                        to = (dx * 4 + dz) * rows
                        stage[to : to + rows, :] = ref[at : at + rows, columns]

        pltpu.make_async_copy(blocks[0].at[0], held.at[slot], sems.at[slot]).wait()
        total[...] += jnp.dot(stage[...], held[slot], preferred_element_type=jnp.float32)
        return carry

    lax.fori_loop(0, live, step, 0)
    for dy in range(4):
        at = pl.multiple_of(s[8 + dy] * 4 * rows, 4 * rows)
        outs[dy][...] = total[pl.ds(at, 4 * rows), :]


def multiply(m, rows, s, lhs, blocks):
    vmem, hbm = pl.BlockSpec(memory_space=pltpu.VMEM), pl.BlockSpec(memory_space=pltpu.HBM)
    return pl.pallas_call(
        functools.partial(multiply_kernel, m, rows),
        in_specs=[pl.BlockSpec(memory_space=pltpu.SMEM)] + [vmem] * 10 + [hbm] * 6,
        out_specs=[vmem] * 4,
        scratch_shapes=[
            pltpu.VMEM((16 * rows, 1024), jnp.bfloat16),
            pltpu.VMEM((4, 1024, 1024), jnp.bfloat16),
            pltpu.VMEM((16 * rows, 1024), jnp.float32),
            pltpu.SemaphoreType.DMA((4,)),
        ],
        out_shape=[jax.ShapeDtypeStruct((4 * rows, 1024), jnp.float32)] * 4,
        compiler_params=pltpu.CompilerParams(vmem_limit_bytes=40 << 20),
        cost_estimate=pl.CostEstimate(
            flops=32 * rows * 1024 * 1024 * m, bytes_accessed=m * (2 << 20) + 32 * rows * 1024 * m, transcendentals=0
        ),
        name="multiply",
    )(s, *lhs, *blocks)


def finish_kernel(rows, s, a, b, c, d, keep, give):
    k = s[0]
    for i in range(2):
        for ref, core in ((keep, k), (give, 1 - k)):
            at = pl.ds(pl.multiple_of(s[12 + 2 * core + i] * rows, rows), rows)
            ref[i] = (a[at, :] + b[at, :] + c[at, :] + d[at, :]).astype(jnp.bfloat16)


def finish(rows, s, parts):
    return pl.pallas_call(
        functools.partial(finish_kernel, rows),
        in_specs=[pl.BlockSpec(memory_space=pltpu.SMEM)] + [pl.BlockSpec(memory_space=pltpu.VMEM)] * 4,
        out_specs=[pl.BlockSpec(memory_space=pltpu.VMEM)] * 2,
        out_shape=[jax.ShapeDtypeStruct((2, rows, 1024), jnp.bfloat16)] * 2,
        compiler_params=pltpu.CompilerParams(vmem_limit_bytes=16 << 20),
        name="finish",
    )(s, *parts)


def first(shard, ring):
    return [shard] + [lax.ppermute(shard, "row", ring(d)) for d in (1, 3, 2)]


def second(line, ring):
    return lax.ppermute(line, "row", ring(1)), lax.ppermute(line, "row", ring(3))


def third(left, right, ring):
    half = left.shape[0] // 2
    return lax.ppermute(left[:half], "row", ring(1)), lax.ppermute(right[half:], "row", ring(3))


def spread(parts, s):
    return [parts[0]] + [lax.ppermute(parts[d], "col", ring_y(d)) for d in (1, 2, 3)]


def body(m, s, integrals, up, down, *blocks):
    other_integrals = lax.ppermute(integrals, "col", SWAP)
    shards, give = tie((pack(m, s, blocks), [up, down]))
    moved = [lax.ppermute(v, "col", ring_y(d)) for v, d in zip(give, (1, 3))]
    rings = ((ring_x, ring_z), (ring_z, ring_x))
    near = [first(shards[h], rings[h][0]) for h in range(2)]
    lines = [[jnp.concatenate([v[a : a + n] for v in near[h]]) for h in range(2)] for a, n in zip(STARTS, ROWS)]
    wide = [second(lines[0][h], rings[h][1]) for h in range(2)]
    wide, late, moved = tie((wide, lines[1], moved))
    across = [third(*wide[h], rings[h][1]) for h in range(2)]
    wide_late = [second(late[h], rings[h][1]) for h in range(2)]
    swapped = [lax.ppermute(v, "col", SWAP) for v in moved]
    blocks = [integrals, other_integrals, moved[0], swapped[0], moved[1], swapped[1]]
    lhs = [v for h in range(2) for v in (lines[0][h], *wide[h], *across[h])]
    parts = multiply(m, ROWS[0], s, lhs, blocks)
    parts, wide_late = tie((parts, wide_late))
    across_late = [third(*wide_late[h], rings[h][1]) for h in range(2)]
    keep0, give0 = finish(ROWS[0], s, spread(parts, s))
    lhs = [v for h in range(2) for v in (late[h], *wide_late[h], *across_late[h])]
    keep1, give1 = finish(ROWS[1], s, spread(multiply(m, ROWS[1], s, lhs, blocks), s))
    mine = jnp.concatenate([keep0, keep1], 1)
    theirs = lax.ppermute(jnp.concatenate([give0, give1], 1), "col", SWAP)
    low = s[0] == 0
    return jnp.stack([jnp.where(low, mine, theirs), jnp.where(low, theirs, mine)], 1).reshape(192, 1024)


def local(amplitudes, integrals, block_counts):
    k = lax.axis_index("col") & 1
    give = lax.dynamic_slice_in_dim(amplitudes, 48 * (1 - k), 48, 0).transpose(1, 0, 2)
    other = lax.ppermute(give, "col", SWAP)
    own = lax.dynamic_slice_in_dim(amplitudes, 48 * k, 48, 0).transpose(1, 0, 2)
    blocks = [own, other]
    for i, d in ((0, 1), (1, 3)):
        blocks.append(lax.ppermute(own[i : i + 1], "col", ring_y(d)))
        blocks.append(lax.ppermute(give[i : i + 1], "col", [(a, b ^ 1) for a, b in ring_y(d)]))
    s = plan(block_counts)
    s, up, down = tie((s, integrals[:1], integrals[1:2]))
    return lax.switch(s[7], [functools.partial(body, m) for m in SIZES], s, integrals, up, down, *blocks)


def solution(mesh):
    return jax.shard_map(
        local,
        mesh=mesh,
        in_specs=(P("row", "col", None), P("col", None, "row"), P()),
        out_specs=P("col", "row"),
        check_vma=False,
    )
```
